32 devices in a mesh: batch: 4 (over y, core), ctx: 8 (over z, x).
Axes of the slice: x: 2, y: 2, z: 4, core: 2. Of those that a mesh axis runs over, the one named last changes fastest.
Arguments:
- activations: bfloat16 [8, 1024, 1024], P('batch', 'ctx'), parts along dimension 0, may hold values from -6 to 6
- project_in: bfloat16 [1024, 3072], replicated, may hold values from -0.1875 to 0.1875
- project_out: bfloat16 [1024, 1024], replicated, may hold values from -0.1875 to 0.1875
- norm_gain: float32 [1024], replicated, may hold values from 0.1 to 1.9
- regularizer: float32 [8, 128], replicated, may hold values from 0.5 to 16
- prior_gram: float32 [32, 128, 128], P('batch'), parts along dimension 0, as said below
- prior_value: float32 [32, 128, 128], P('batch'), parts along dimension 0, as said below
Outputs:
- layer_out: bfloat16 [8, 1024, 1024], P('batch', 'ctx'), parts along dimension 0
- next_gram: float32 [32, 128, 128], P('batch'), parts along dimension 0
- next_value: float32 [32, 128, 128], P('batch'), parts along dimension 0
The draws below stay inside these ranges and needn't reach their ends.
There are 4 independent parts, one for each index of `batch`. The reference program is written for one: setup_inputs(seed, part) draws one part's arguments, and reference() takes and returns one part's arrays. A program takes and returns all parts, laid end to end along the dimension named above; an argument that names none is the same for every part. Nothing has to cross between parts.
Inputs may be any that keep to these rules, and one draw needn't show every extreme that they name: `prior_gram`: each head's matrix is symmetric positive definite. `prior_value`: summed over the same earlier tokens as prior_gram.
All inputs are finite; a program needn't handle non-finite values.
Results may differ from the reference program's by a relative error of at most 0.0055.
Values sent between devices are 32-bit elements; how exact they have to be, the bound alone decides.
A program may use at most 128 MiB of HBM per device.

```python
import math
import jax
import jax.numpy as jnp
from jax import lax

D = 1024
HEADS = 8
DK = 128
TOK_DEV = 128
SEGS = 2
ITERS = 8
SEG_LEN = 1024


def prior_parts(key):
    base = jax.random.fold_in(key, 7)
    first_key, second_key = jax.random.split(base)
    keys_prior = jax.random.normal(first_key, (HEADS, DK, 2 * DK), jnp.float32) * 0.35
    values_prior = jax.random.normal(second_key, (HEADS, DK, 2 * DK), jnp.float32) * 0.35
    return (keys_prior, values_prior)


def draw_prior_gram(key, part):
    keys_prior, values_prior = prior_parts(key)
    return jnp.einsum('hin,hjn->hij', keys_prior, keys_prior)


def draw_prior_value(key, part):
    keys_prior, values_prior = prior_parts(key)
    return jnp.einsum('hin,hjn->hij', values_prior, keys_prior)


def block_levels(key, extent, pieces, smallest, top_value):
    loudness, own = 1.0, jax.random.fold_in(key, 6)
    for axis_at, blocks in pieces:
        steps = jnp.exp(jax.random.uniform(jax.random.fold_in(own, axis_at), (blocks,), jnp.float32, smallest / len(pieces), top_value / len(pieces)))
        loudness = loudness * jnp.repeat(steps, extent[axis_at] // blocks).reshape([-1 if axis == axis_at else 1 for axis in range(len(extent))])
    return loudness


def normal_values(stream_key, shape, scale, reach, cuts=(), held_as=jnp.bfloat16):
    level = block_levels(stream_key, shape, cuts, -0.22, 0.18) if cuts else 1.0
    array = jax.random.normal(stream_key, shape, jnp.float32) * scale * level
    return jnp.minimum(jnp.maximum(array, -reach), reach).astype(held_as)


def setup_inputs(seed: int = 0, part: int = 0) -> dict:
    streams_of = jax.random.split(jax.random.key(seed), 8)
    part_keys = jax.random.split(jax.random.fold_in(streams_of[7], part), 8)
    return {
        "activations": normal_values(part_keys[0], (SEGS, SEG_LEN, D), 1.0, 6.0, ((1, 8),)),
        "project_in": normal_values(streams_of[1], (D, 3 * D), D ** -0.5, 0.1875),
        "project_out": normal_values(streams_of[2], (D, D), D ** -0.5, 0.1875),
        "norm_gain": jnp.clip(1.0 + 0.18 * jax.random.normal(streams_of[3], (D,), jnp.float32), 0.1, 1.9),
        "regularizer": jnp.clip(jnp.exp(jax.random.uniform(streams_of[4], (HEADS, DK), jnp.float32, math.log(0.5), math.log(16.0))), 0.5, 16.0),
        "prior_gram": draw_prior_gram(jax.random.fold_in(jax.random.fold_in(streams_of[7], part), 71), part),
        "prior_value": draw_prior_value(jax.random.fold_in(jax.random.fold_in(streams_of[7], part), 71), part),
    }


epsilon = 1e-06
highest = lax.Precision.HIGHEST

def split_heads(packed):
    lead = packed.shape[:-1]
    parts = packed.reshape(lead + (3, HEADS, DK))
    parts = jnp.moveaxis(parts, -3, 0)
    parts = jnp.swapaxes(parts, -3, -2)
    return (parts[0], parts[1], parts[2])

def unit_rows(matrix):
    return matrix * lax.rsqrt(lax.optimization_barrier(jnp.sum(matrix * matrix, -1, keepdims=True)) + epsilon)

def mesa_block(queries, keys_unit, values, gram_state, value_state, regularizer):
    block_len = queries.shape[-2]
    row_index = lax.broadcasted_iota(jnp.int32, (block_len, block_len), 0)
    col_index = lax.broadcasted_iota(jnp.int32, (block_len, block_len), 1)
    causal = (row_index >= col_index).astype(jnp.float32)
    diag_reg = regularizer[:, None, :]

    def apply_gram(direction):
        earlier = jnp.einsum('...ij,...tj->...ti', gram_state, direction, precision=highest)
        scores = jnp.einsum('...ti,...si->...ts', direction, keys_unit, precision=highest) * causal
        return earlier + diag_reg * direction + jnp.einsum('...ts,...si->...ti', scores, keys_unit, precision=highest)
    solution = jnp.zeros_like(queries)
    residual = queries
    direction = queries
    norm_now = lax.optimization_barrier(jnp.sum(residual * residual, -1, keepdims=True))
    for repeat in range(ITERS):
        gram_image = apply_gram(direction)
        step_size = norm_now / (lax.optimization_barrier(jnp.sum(direction * gram_image, -1, keepdims=True)) + epsilon)
        solution = solution + step_size * direction
        residual = residual - step_size * gram_image
        norm_next = lax.optimization_barrier(jnp.sum(residual * residual, -1, keepdims=True))
        direction = residual + norm_next / (norm_now + epsilon) * direction
        norm_now = norm_next
    earlier = jnp.einsum('...ij,...tj->...ti', value_state, solution, precision=highest)
    scores = jnp.einsum('...ti,...si->...ts', solution, keys_unit, precision=highest) * causal
    return earlier + jnp.einsum('...ts,...si->...ti', scores, values, precision=highest)

def finish(mixed, norm_gain):
    scaled = mixed * lax.rsqrt(lax.optimization_barrier(jnp.mean(mixed * mixed, -1, keepdims=True)) + epsilon)
    scaled = jnp.swapaxes(scaled, -3, -2)
    merged = scaled.reshape(scaled.shape[:-2] + (HEADS * DK,))
    return (merged * norm_gain).astype(jnp.bfloat16)

def reference(activations, project_in, project_out, norm_gain, regularizer, prior_gram, prior_value):
    width = activations.shape[-1]
    blocks = activations.reshape(SEGS * SEG_LEN // TOK_DEV, TOK_DEV, width)

    def block_step(carry, block):
        gram_state, value_state = carry
        packed = jnp.dot(block, project_in, preferred_element_type=jnp.float32)
        queries, keys_unit, values = split_heads(packed)
        queries = unit_rows(queries)
        keys_unit = unit_rows(keys_unit)
        mixed = mesa_block(queries, keys_unit, values, gram_state, value_state, regularizer)
        normed = finish(mixed, norm_gain)
        result = jnp.dot(normed, project_out, preferred_element_type=jnp.float32).astype(jnp.bfloat16)
        gram_state = gram_state + jnp.einsum('hti,htj->hij', keys_unit, keys_unit, precision=highest)
        value_state = value_state + jnp.einsum('hti,htj->hij', values, keys_unit, precision=highest)
        return ((gram_state, value_state), result)
    (gram_final, value_final), outputs = lax.scan(block_step, (prior_gram, prior_value), blocks)
    return (outputs.reshape(activations.shape), gram_final, value_final)
```

```python
import functools

import jax
import jax.numpy as jnp
from jax import lax
from jax.experimental import pallas as pl
from jax.experimental.pallas import tpu as pltpu
from jax.sharding import PartitionSpec as P

ITERS = 8
epsilon = 1e-06
f32, bf16 = jnp.float32, jnp.bfloat16
GROUP = 2


def halves(m):
    high = m.astype(bf16)
    return high, (m - high.astype(f32)).astype(bf16)


def left_of(m):
    return jnp.concatenate(halves(m), axis=1)


def right_of(m):
    high, low = halves(m)
    top = jnp.concatenate([high, low], axis=1)
    return jnp.concatenate([top, jnp.concatenate([high, jnp.zeros_like(low)], axis=1)], axis=0)


def product(left, right):
    n = right.shape[1] // 2
    wide = jnp.dot(left, right, preferred_element_type=f32)
    return wide[:, :n] + wide[:, n:]


def unit_rows(m):
    return m * lax.rsqrt(jnp.sum(m * m, -1, keepdims=True) + epsilon)


def kernel(
    near, far, heads, dk, segs,
    x_ref, win_ref, wout_ref, gain_ref, reg_ref, pg_ref, pv_ref,
    out_ref, ng_ref, nv_ref,
    win, wout, k_left, kt_left, vt_left, q_t,
    own_g, own_v, near_g, near_v, sum_g, sum_v, got_g, got_v, put_g, put_v,
    sol, res, dirn, rr_ref, ak_left, x_right, part, normed,
    copy_sem, near_send, near_recv, far_send, far_recv,
):
    width = heads * dk
    tok = x_ref.shape[0] // segs
    me = lax.axis_index("ctx")
    slow, fast = me // near, me % near
    first = (2 * slow >= far).astype(jnp.int32)

    copies = [
        pltpu.make_async_copy(
            win_ref.at[:, pl.ds(c * width, width)], win.at[:, pl.ds(c * width, width)], copy_sem.at[c]
        )
        for c in range(3)
    ]
    copies.append(pltpu.make_async_copy(wout_ref, wout, copy_sem.at[3]))
    for c in (1, 2, 0, 3):
        copies[c].start()

    barrier = pltpu.get_barrier_semaphore()
    for off in range(1, near):
        pl.semaphore_signal(barrier, inc=1, device_id={"ctx": slow * near + (fast + off) % near})

    @pl.when(slow > 0)
    def _():
        pl.semaphore_signal(barrier, inc=1, device_id={"ctx": me - near})

    @pl.when(slow < far - 1)
    def _():
        pl.semaphore_signal(barrier, inc=1, device_id={"ctx": me + near})

    ends = (slow > 0).astype(jnp.int32) + (slow < far - 1).astype(jnp.int32)
    pl.semaphore_wait(barrier, near - 1 + ends)

    own, nears, sums = (own_g, own_v), (near_g, near_v), (sum_g, sum_v)
    got, put = (got_g, got_v), (put_g, put_v)

    for kind in range(2):
        @pl.when(slow == 0)
        def _():
            got[kind][0] = jnp.zeros(got[kind].shape[1:], f32)

        @pl.when(slow == far - 1)
        def _():
            got[kind][1] = jnp.zeros(got[kind].shape[1:], f32)

    def near_copy(kind, h, off):
        slot = near - off - 1
        return pltpu.make_async_remote_copy(
            src_ref=own[kind].at[h],
            dst_ref=nears[kind].at[slot, h],
            send_sem=near_send.at[kind, slot, h],
            recv_sem=near_recv.at[kind, slot, h],
            device_id={"ctx": slow * near + (fast + off) % near},
        )

    def far_copy(kind, h, way, peer):
        return pltpu.make_async_remote_copy(
            src_ref=put[kind].at[way, h],
            dst_ref=got[kind].at[way, h],
            send_sem=far_send.at[kind, way, h],
            recv_sem=far_recv.at[kind, way, h],
            device_id={"ctx": peer},
        )

    def relay(kind, h, stage):
        way = first if stage == 0 else 1 - first
        step = 1 - 2 * way
        if stage == 0:
            total = own[kind][h]
            for off in range(1, near):
                near_copy(kind, h, off).wait_recv()
            for slot in range(near - 1):
                total = total + nears[kind][slot, h]
            sums[kind][h] = total
        before, after = slow - step, slow + step

        @pl.when((before >= 0) & (before < far))
        def _():
            far_copy(kind, h, way, me - step * near).wait_recv()

        @pl.when((after >= 0) & (after < far))
        def _():
            put[kind][way, h] = got[kind][way, h] + sums[kind][h]
            far_copy(kind, h, way, me + step * near).start()

    def prefix_and_total(kind, h):
        forward, backward = got[kind][0, h], got[kind][1, h]
        ahead = forward
        for slot in range(near - 1):
            weight = (fast + slot + 1 >= near).astype(f32)
            ahead = ahead + weight * nears[kind][slot, h]
        return ahead, forward + sums[kind][h] + backward

    row = lax.broadcasted_iota(jnp.int32, (dk, dk), 0)
    col = lax.broadcasted_iota(jnp.int32, (dk, dk), 1)
    lower, diagonal = row >= col, row == col
    trow = lax.broadcasted_iota(jnp.int32, (tok, tok), 0)
    tcol = lax.broadcasted_iota(jnp.int32, (tok, tok), 1)
    causal = trow <= tcol

    def unpack(p):
        body, tail = p[:dk], p[dk : dk + 1]
        turned = body.T
        zero = jnp.where(lower, body, turned)
        one = jnp.where(diagonal, tail, jnp.where(lower, turned, body))
        return zero, one

    copies[1].wait()

    def keys_step(p, c):
        at = pl.multiple_of(p * (GROUP * dk), GROUP * dk)
        keys = jnp.dot(x_ref[...], win[:, pl.ds(width + at, GROUP * dk)], preferred_element_type=f32)
        for g in range(GROUP):
            h = p * GROUP + g
            grams = []
            for s in range(segs):
                unit = unit_rows(keys[s * tok : (s + 1) * tok, g * dk : (g + 1) * dk])
                kt = left_of(unit.T)
                k_left[h, s] = left_of(unit)
                kt_left[h, s] = kt
                grams.append(product(kt, right_of(unit)))
            own_g[h, :dk] = jnp.where(lower, grams[0], grams[1])
            tail = jnp.sum(jnp.where(diagonal, grams[1], 0.0), axis=0, keepdims=True)
            own_g[h, dk:] = jnp.broadcast_to(tail, (8, dk))
            for off in range(1, near):
                near_copy(0, h, off).start()
        return c

    lax.fori_loop(0, heads // GROUP, keys_step, 0)
    copies[2].wait()
    copies[0].wait()

    def rest_step(p, c):
        at = pl.multiple_of(p * (GROUP * dk), GROUP * dk)
        values = jnp.dot(x_ref[...], win[:, pl.ds(2 * width + at, GROUP * dk)], preferred_element_type=f32)
        queries = jnp.dot(x_ref[...], win[:, pl.ds(at, GROUP * dk)], preferred_element_type=f32)
        for g in range(GROUP):
            h = p * GROUP + g
            for s in range(segs):
                rows, lanes = slice(s * tok, (s + 1) * tok), slice(g * dk, (g + 1) * dk)
                vt = left_of(values[rows, lanes].T)
                vt_left[h, s] = vt
                both = k_left[h, s]
                high, low = both[:, :dk], both[:, dk:]
                right = jnp.concatenate(
                    [both, jnp.concatenate([high, jnp.zeros_like(low)], axis=1)], axis=0
                )
                own_v[h, s * dk : (s + 1) * dk] = product(vt, right)
                q_t[h, s] = unit_rows(queries[rows, lanes]).T
            for off in range(1, near):
                near_copy(1, h, off).start()
        return c

    lax.fori_loop(0, heads // GROUP, rest_step, 0)

    def each(kind, stage, lo, count):
        def go(i, c):
            relay(kind, lo + i, stage)
            return c

        lax.fori_loop(0, count, go, 0)

    each(0, 0, 0, heads)
    each(0, 1, 0, GROUP)

    def solve_step(p, c):
        for g in range(GROUP):
            h = p * GROUP + g
            ahead, total = prefix_and_total(0, h)
            ahead0, ahead1 = unpack(ahead)
            total0, total1 = unpack(total)
            prior = pg_ref[h]
            ng_ref[h] = prior + (total0 + total1)
            diag = jnp.where(diagonal, reg_ref[pl.ds(h, 1), :], 0.0)
            base = prior + diag
            for s, gram in enumerate((base + ahead0, base + (total0 + ahead1))):
                i = g * segs + s
                ak_left[i, :dk] = left_of(gram)
                ak_left[i, dk:] = k_left[h, s]
                q = q_t[h, s]
                sol[i] = jnp.zeros_like(q)
                res[i] = q
                dirn[i] = q
                rr_ref[i] = jnp.broadcast_to(jnp.sum(q * q, 0, keepdims=True), rr_ref.shape[1:])

        def cg(it, c2):
            for g in range(GROUP):
                h = p * GROUP + g
                for s in range(segs):
                    i = g * segs + s
                    d = dirn[i]
                    y = product(ak_left[i], right_of(d))
                    scores = jnp.where(causal, y[dk:], 0.0)
                    image = y[:dk] + product(kt_left[h, s], right_of(scores))
                    rr = rr_ref[i, 0:1]
                    step = rr / (jnp.sum(d * image, 0, keepdims=True) + epsilon)
                    sol[i] = sol[i] + step * d
                    r = res[i] - step * image
                    res[i] = r
                    new = jnp.sum(r * r, 0, keepdims=True)
                    dirn[i] = r + (new / (rr + epsilon)) * d
                    rr_ref[i] = jnp.broadcast_to(new, rr_ref.shape[1:])
            return c2

        lax.fori_loop(0, ITERS, cg, 0)
        for g in range(GROUP):
            h = p * GROUP + g
            for s in range(segs):
                right = right_of(sol[g * segs + s])
                x_right[h, s] = right
                scores = jnp.where(causal, product(k_left[h, s], right), 0.0)
                part[h, s] = product(vt_left[h, s], right_of(scores))

        @pl.when(p < heads // GROUP - 1)
        def _():
            each(0, 1, (p + 1) * GROUP, GROUP)

        each(1, 0, p * GROUP, GROUP)

        @pl.when(p > 0)
        def _():
            each(1, 1, (p - 1) * GROUP, GROUP)

        return c

    lax.fori_loop(0, heads // GROUP, solve_step, 0)
    each(1, 1, heads - GROUP, GROUP)

    def mix_step(h, c):
        ahead, total = prefix_and_total(1, h)
        prior = pv_ref[h]
        total0 = total[:dk]
        nv_ref[h] = prior + (total0 + total[dk:])
        at = pl.multiple_of(h * dk, dk)
        for s, value in enumerate((prior + ahead[:dk], prior + (total0 + ahead[dk:]))):
            mixed = product(left_of(value), x_right[h, s]) + part[h, s]
            mean = jnp.sum(mixed * mixed, 0, keepdims=True) / dk
            scaled = (mixed * lax.rsqrt(mean + epsilon)).T * gain_ref[pl.ds(h, 1), :]
            normed[s * tok : (s + 1) * tok, pl.ds(at, dk)] = scaled.astype(bf16)
        return c

    lax.fori_loop(0, heads, mix_step, 0)
    copies[3].wait()
    out_ref[...] = jnp.dot(normed[...], wout[...], preferred_element_type=f32).astype(bf16)

    def drain(h, c):
        for kind in range(2):
            for off in range(1, near):
                near_copy(kind, h, off).wait_send()

            @pl.when(slow < far - 1)
            def _():
                far_copy(kind, h, 0, me + near).wait_send()

            @pl.when(slow > 0)
            def _():
                far_copy(kind, h, 1, me - near).wait_send()

        return c

    lax.fori_loop(0, heads, drain, 0)


def solution(mesh):
    n = mesh.shape["ctx"]
    near = 1 << ((n.bit_length() - 1) // 2)
    far = n // near

    def shards(activations, project_in, project_out, norm_gain, regularizer, prior_gram, prior_value):
        segs, tok, width = activations.shape
        heads, dk = regularizer.shape
        feats = heads * dk
        chains = GROUP * segs
        vmem = pl.BlockSpec(memory_space=pltpu.VMEM)
        hbm = pl.BlockSpec(memory_space=pl.ANY)
        gram, value = (dk + 8, dk), (segs * dk, dk)
        V = pltpu.VMEM
        D = pltpu.SemaphoreType.DMA
        slots = max(near - 1, 1)
        out, ng, nv = pl.pallas_call(
            functools.partial(kernel, near, far, heads, dk, segs),
            out_shape=(
                jax.ShapeDtypeStruct((segs * tok, width), bf16),
                jax.ShapeDtypeStruct(prior_gram.shape, f32),
                jax.ShapeDtypeStruct(prior_value.shape, f32),
            ),
            in_specs=[vmem, hbm, hbm, vmem, vmem, vmem, vmem],
            out_specs=(vmem, vmem, vmem),
            scratch_shapes=[
                V(project_in.shape, bf16),
                V(project_out.shape, bf16),
                V((heads, segs, tok, 2 * dk), bf16),
                V((heads, segs, dk, 2 * tok), bf16),
                V((heads, segs, dk, 2 * tok), bf16),
                V((heads, segs, dk, tok), f32),
                V((heads,) + gram, f32),
                V((heads,) + value, f32),
                V((slots, heads) + gram, f32),
                V((slots, heads) + value, f32),
                V((heads,) + gram, f32),
                V((heads,) + value, f32),
                V((2, heads) + gram, f32),
                V((2, heads) + value, f32),
                V((2, heads) + gram, f32),
                V((2, heads) + value, f32),
                V((chains, dk, tok), f32),
                V((chains, dk, tok), f32),
                V((chains, dk, tok), f32),
                V((chains, 8, tok), f32),
                V((chains, dk + tok, 2 * dk), bf16),
                V((heads, segs, 2 * dk, 2 * tok), bf16),
                V((heads, segs, dk, tok), f32),
                V((segs * tok, feats), bf16),
                D((4,)),
                D((2, slots, heads)),
                D((2, slots, heads)),
                D((2, 2, heads)),
                D((2, 2, heads)),
            ],
            compiler_params=pltpu.CompilerParams(
                collective_id=0, has_side_effects=True, vmem_limit_bytes=60 << 20
            ),
        )(
            activations.reshape(segs * tok, width),
            project_in,
            project_out,
            norm_gain.reshape(heads, dk),
            regularizer,
            prior_gram,
            prior_value,
        )
        return out.reshape(activations.shape), ng, nv

    return jax.shard_map(
        shards,
        mesh=mesh,
        in_specs=(
            P("batch", "ctx", None), P(), P(), P(), P(),
            P("batch", None, None), P("batch", None, None),
        ),
        out_specs=(P("batch", "ctx", None), P("batch", None, None), P("batch", None, None)),
        check_vma=False,
    )
```

```python
import functools

import jax
import jax.numpy as jnp
from jax import lax
from jax.experimental import pallas as pl
from jax.experimental.pallas import tpu as pltpu
from jax.sharding import PartitionSpec as P

ITERS = 8
epsilon = 1e-06
f32, bf16 = jnp.float32, jnp.bfloat16
GROUP = 2


def halves(m):
    high = m.astype(bf16)
    return high, (m - high.astype(f32)).astype(bf16)


def left_of(m):
    return jnp.concatenate(halves(m), axis=1)


def right_of(m):
    high, low = halves(m)
    top = jnp.concatenate([high, low], axis=1)
    return jnp.concatenate([top, jnp.concatenate([high, jnp.zeros_like(low)], axis=1)], axis=0)


def product(left, right):
    n = right.shape[1] // 2
    wide = jnp.dot(left, right, preferred_element_type=f32)
    return wide[:, :n] + wide[:, n:]


def unit_rows(m):
    return m * lax.rsqrt(jnp.sum(m * m, -1, keepdims=True) + epsilon)


def kernel(
    near, far, heads, dk, segs,
    x_ref, win_ref, wout_ref, gain_ref, reg_ref, pg_ref, pv_ref,
    out_ref, ng_ref, nv_ref,
    win, wout, k_left, kt_left, vt_left, q_t,
    own_g, own_v, near_g, near_v, sum_g, sum_v, got_g, got_v, put_g, put_v,
    sol, res, dirn, rr_ref, ak_left, x_right, part, normed,
    copy_sem, near_send, near_recv, far_send, far_recv,
):
    width = heads * dk
    tok = x_ref.shape[0] // segs
    me = lax.axis_index("ctx")
    slow, fast = me // near, me % near
    first = (2 * slow >= far).astype(jnp.int32)

    copies = [
        pltpu.make_async_copy(
            win_ref.at[:, pl.ds(c * width, width)], win.at[:, pl.ds(c * width, width)], copy_sem.at[c]
        )
        for c in range(3)
    ]
    copies.append(pltpu.make_async_copy(wout_ref, wout, copy_sem.at[3]))
    for c in (1, 2, 0, 3):
        copies[c].start()

    barrier = pltpu.get_barrier_semaphore()
    for off in range(1, near):
        pl.semaphore_signal(barrier, inc=1, device_id={"ctx": slow * near + (fast + off) % near})

    @pl.when(slow > 0)
    def _():
        pl.semaphore_signal(barrier, inc=1, device_id={"ctx": me - near})

    @pl.when(slow < far - 1)
    def _():
        pl.semaphore_signal(barrier, inc=1, device_id={"ctx": me + near})

    ends = (slow > 0).astype(jnp.int32) + (slow < far - 1).astype(jnp.int32)
    pl.semaphore_wait(barrier, near - 1 + ends)

    own, nears, sums = (own_g, own_v), (near_g, near_v), (sum_g, sum_v)
    got, put = (got_g, got_v), (put_g, put_v)

    for kind in range(2):
        @pl.when(slow == 0)
        def _():
            got[kind][0] = jnp.zeros(got[kind].shape[1:], f32)

        @pl.when(slow == far - 1)
        def _():
            got[kind][1] = jnp.zeros(got[kind].shape[1:], f32)

    def near_copy(kind, h, off):
        slot = near - off - 1
        return pltpu.make_async_remote_copy(
            src_ref=own[kind].at[h],
            dst_ref=nears[kind].at[slot, h],
            send_sem=near_send.at[kind, slot, h],
            recv_sem=near_recv.at[kind, slot, h],
            device_id={"ctx": slow * near + (fast + off) % near},
        )

    def far_copy(kind, h, way, peer):
        return pltpu.make_async_remote_copy(
            src_ref=put[kind].at[way, h],
            dst_ref=got[kind].at[way, h],
            send_sem=far_send.at[kind, way, h],
            recv_sem=far_recv.at[kind, way, h],
            device_id={"ctx": peer},
        )

    def relay(kind, h, stage):
        way = first if stage == 0 else 1 - first
        step = 1 - 2 * way
        if stage == 0:
            total = own[kind][h]
            for off in range(1, near):
                near_copy(kind, h, off).wait_recv()
            for slot in range(near - 1):
                total = total + nears[kind][slot, h]
            sums[kind][h] = total
        before, after = slow - step, slow + step
        passes = (after >= 0) & (after < far)
        waits = (before >= 0) & (before < far)

        @pl.when(waits & passes if stage else waits)
        def _():
            far_copy(kind, h, way, me - step * near).wait_recv()

        @pl.when(passes)
        def _():
            put[kind][way, h] = got[kind][way, h] + sums[kind][h]
            far_copy(kind, h, way, me + step * near).start()

    def prefix_and_total(kind, h):
        way = 1 - first
        step = 1 - 2 * way
        before, after = slow - step, slow + step

        @pl.when((before >= 0) & (before < far) & ((after < 0) | (after >= far)))
        def _():
            far_copy(kind, h, way, me - step * near).wait_recv()

        forward, backward = got[kind][0, h], got[kind][1, h]
        ahead = forward
        for slot in range(near - 1):
            weight = (fast + slot + 1 >= near).astype(f32)
            ahead = ahead + weight * nears[kind][slot, h]
        return ahead, forward + sums[kind][h] + backward

    row = lax.broadcasted_iota(jnp.int32, (dk, dk), 0)
    col = lax.broadcasted_iota(jnp.int32, (dk, dk), 1)
    lower, diagonal = row >= col, row == col
    trow = lax.broadcasted_iota(jnp.int32, (tok, tok), 0)
    tcol = lax.broadcasted_iota(jnp.int32, (tok, tok), 1)
    causal = trow <= tcol

    def unpack(p):
        body, tail = p[:dk], p[dk : dk + 1]
        turned = body.T
        zero = jnp.where(lower, body, turned)
        one = jnp.where(diagonal, tail, jnp.where(lower, turned, body))
        return zero, one

    early = heads // 2
    copies[1].wait()

    def keys_step(p, c):
        at = pl.multiple_of(p * (GROUP * dk), GROUP * dk)
        keys = jnp.dot(x_ref[...], win[:, pl.ds(width + at, GROUP * dk)], preferred_element_type=f32)
        for g in range(GROUP):
            h = p * GROUP + g
            grams = []
            for s in range(segs):
                unit = unit_rows(keys[s * tok : (s + 1) * tok, g * dk : (g + 1) * dk])
                kt = left_of(unit.T)
                k_left[h, s] = left_of(unit)
                kt_left[h, s] = kt
                grams.append(product(kt, right_of(unit)))
            own_g[h, :dk] = jnp.where(lower, grams[0], grams[1])
            tail = jnp.sum(jnp.where(diagonal, grams[1], 0.0), axis=0, keepdims=True)
            own_g[h, dk:] = jnp.broadcast_to(tail, (8, dk))
            for off in range(1, near):
                near_copy(0, h, off).start()
        return c

    lax.fori_loop(0, heads // GROUP, keys_step, 0)
    copies[2].wait()
    copies[0].wait()

    def rest_step(p, c):
        at = pl.multiple_of(p * (GROUP * dk), GROUP * dk)
        values = jnp.dot(x_ref[...], win[:, pl.ds(2 * width + at, GROUP * dk)], preferred_element_type=f32)
        queries = jnp.dot(x_ref[...], win[:, pl.ds(at, GROUP * dk)], preferred_element_type=f32)
        for g in range(GROUP):
            h = p * GROUP + g
            for s in range(segs):
                rows, lanes = slice(s * tok, (s + 1) * tok), slice(g * dk, (g + 1) * dk)
                vt = left_of(values[rows, lanes].T)
                vt_left[h, s] = vt
                both = k_left[h, s]
                high, low = both[:, :dk], both[:, dk:]
                right = jnp.concatenate(
                    [both, jnp.concatenate([high, jnp.zeros_like(low)], axis=1)], axis=0
                )
                own_v[h, s * dk : (s + 1) * dk] = product(vt, right)
                q_t[h, s] = unit_rows(queries[rows, lanes]).T
            for off in range(1, near):
                near_copy(1, h, off).start()
        return c

    lax.fori_loop(0, heads // GROUP, rest_step, 0)

    def each(kind, stage, lo, count):
        def go(i, c):
            relay(kind, lo + i, stage)
            return c

        lax.fori_loop(0, count, go, 0)

    each(0, 0, 0, early)
    each(0, 1, 0, GROUP)

    def service(n):
        @pl.when(n < heads - early)
        def _():
            relay(0, early + n, 0)

        @pl.when(n < heads - GROUP)
        def _():
            relay(0, GROUP + n, 1)

        @pl.when((n >= ITERS) & (n % 2 == 0) & (n < ITERS + 2 * heads))
        def _():
            relay(1, (n - ITERS) // 2, 0)

        late = n - ITERS - 5

        @pl.when((late >= 0) & (late % 2 == 0) & (late < 2 * heads))
        def _():
            relay(1, late // 2, 1)

    def solve_step(p, c):
        for g in range(GROUP):
            h = p * GROUP + g
            ahead, total = prefix_and_total(0, h)
            ahead0, ahead1 = unpack(ahead)
            total0, total1 = unpack(total)
            prior = pg_ref[h]
            ng_ref[h] = prior + (total0 + total1)
            diag = jnp.where(diagonal, reg_ref[pl.ds(h, 1), :], 0.0)
            base = prior + diag
            for s, gram in enumerate((base + ahead0, base + (total0 + ahead1))):
                i = g * segs + s
                ak_left[i, :dk] = left_of(gram)
                ak_left[i, dk:] = k_left[h, s]
                q = q_t[h, s]
                sol[i] = jnp.zeros_like(q)
                res[i] = q
                dirn[i] = q
                rr_ref[i] = jnp.broadcast_to(jnp.sum(q * q, 0, keepdims=True), rr_ref.shape[1:])

        def cg(it, c2):
            for g in range(GROUP):
                h = p * GROUP + g
                for s in range(segs):
                    i = g * segs + s
                    d = dirn[i]
                    y = product(ak_left[i], right_of(d))
                    scores = jnp.where(causal, y[dk:], 0.0)
                    image = y[:dk] + product(kt_left[h, s], right_of(scores))
                    rr = rr_ref[i, 0:1]
                    step = rr / (jnp.sum(d * image, 0, keepdims=True) + epsilon)
                    sol[i] = sol[i] + step * d
                    r = res[i] - step * image
                    res[i] = r
                    new = jnp.sum(r * r, 0, keepdims=True)
                    dirn[i] = r + (new / (rr + epsilon)) * d
                    rr_ref[i] = jnp.broadcast_to(new, rr_ref.shape[1:])
            service(p * ITERS + it)
            return c2

        lax.fori_loop(0, ITERS, cg, 0)
        for g in range(GROUP):
            h = p * GROUP + g
            for s in range(segs):
                right = right_of(sol[g * segs + s])
                x_right[h, s] = right
                scores = jnp.where(causal, product(k_left[h, s], right), 0.0)
                part[h, s] = product(vt_left[h, s], right_of(scores))

        return c

    lax.fori_loop(0, heads // GROUP, solve_step, 0)

    def mix_step(h, c):
        ahead, total = prefix_and_total(1, h)
        prior = pv_ref[h]
        total0 = total[:dk]
        nv_ref[h] = prior + (total0 + total[dk:])
        at = pl.multiple_of(h * dk, dk)
        for s, value in enumerate((prior + ahead[:dk], prior + (total0 + ahead[dk:]))):
            mixed = product(left_of(value), x_right[h, s]) + part[h, s]
            mean = jnp.sum(mixed * mixed, 0, keepdims=True) / dk
            scaled = (mixed * lax.rsqrt(mean + epsilon)).T * gain_ref[pl.ds(h, 1), :]
            normed[s * tok : (s + 1) * tok, pl.ds(at, dk)] = scaled.astype(bf16)
        return c

    lax.fori_loop(0, heads, mix_step, 0)
    copies[3].wait()
    out_ref[...] = jnp.dot(normed[...], wout[...], preferred_element_type=f32).astype(bf16)

    def drain(h, c):
        for kind in range(2):
            for off in range(1, near):
                near_copy(kind, h, off).wait_send()

            @pl.when(slow < far - 1)
            def _():
                far_copy(kind, h, 0, me + near).wait_send()

            @pl.when(slow > 0)
            def _():
                far_copy(kind, h, 1, me - near).wait_send()

        return c

    lax.fori_loop(0, heads, drain, 0)


def solution(mesh):
    n = mesh.shape["ctx"]
    near = 1 << ((n.bit_length() - 1) // 2)
    far = n // near

    def shards(activations, project_in, project_out, norm_gain, regularizer, prior_gram, prior_value):
        segs, tok, width = activations.shape
        heads, dk = regularizer.shape
        feats = heads * dk
        chains = GROUP * segs
        vmem = pl.BlockSpec(memory_space=pltpu.VMEM)
        hbm = pl.BlockSpec(memory_space=pl.ANY)
        gram, value = (dk + 8, dk), (segs * dk, dk)
        V = pltpu.VMEM
        D = pltpu.SemaphoreType.DMA
        slots = max(near - 1, 1)
        out, ng, nv = pl.pallas_call(
            functools.partial(kernel, near, far, heads, dk, segs),
            out_shape=(
                jax.ShapeDtypeStruct((segs * tok, width), bf16),
                jax.ShapeDtypeStruct(prior_gram.shape, f32),
                jax.ShapeDtypeStruct(prior_value.shape, f32),
            ),
            in_specs=[vmem, hbm, hbm, vmem, vmem, vmem, vmem],
            out_specs=(vmem, vmem, vmem),
            scratch_shapes=[
                V(project_in.shape, bf16),
                V(project_out.shape, bf16),
                V((heads, segs, tok, 2 * dk), bf16),
                V((heads, segs, dk, 2 * tok), bf16),
                V((heads, segs, dk, 2 * tok), bf16),
                V((heads, segs, dk, tok), f32),
                V((heads,) + gram, f32),
                V((heads,) + value, f32),
                V((slots, heads) + gram, f32),
                V((slots, heads) + value, f32),
                V((heads,) + gram, f32),
                V((heads,) + value, f32),
                V((2, heads) + gram, f32),
                V((2, heads) + value, f32),
                V((2, heads) + gram, f32),
                V((2, heads) + value, f32),
                V((chains, dk, tok), f32),
                V((chains, dk, tok), f32),
                V((chains, dk, tok), f32),
                V((chains, 8, tok), f32),
                V((chains, dk + tok, 2 * dk), bf16),
                V((heads, segs, 2 * dk, 2 * tok), bf16),
                V((heads, segs, dk, tok), f32),
                V((segs * tok, feats), bf16),
                D((4,)),
                D((2, slots, heads)),
                D((2, slots, heads)),
                D((2, 2, heads)),
                D((2, 2, heads)),
            ],
            compiler_params=pltpu.CompilerParams(
                collective_id=0, has_side_effects=True, vmem_limit_bytes=60 << 20
            ),
        )(
            activations.reshape(segs * tok, width),
            project_in,
            project_out,
            norm_gain.reshape(heads, dk),
            regularizer,
            prior_gram,
            prior_value,
        )
        return out.reshape(activations.shape), ng, nv

    return jax.shard_map(
        shards,
        mesh=mesh,
        in_specs=(
            P("batch", "ctx", None), P(), P(), P(), P(),
            P("batch", None, None), P("batch", None, None),
        ),
        out_specs=(P("batch", "ctx", None), P("batch", None, None), P("batch", None, None)),
        check_vma=False,
    )
```
